512 devices in a mesh: mom: 8 (over z_lo), en: 64 (over z_hi, y, x, core).
Axes of the slice: x: 4, y: 4, z: 16 (z_hi: 2, z_lo: 8; z = z_hi * 8 + z_lo), core: 2. Of those that a mesh axis runs over, the one named last changes fastest.
Arguments:
- green: bfloat16 [8, 512, 2, 2, 64, 128], P('mom', 'en'), may hold values from -6 to 6
- pair_index: int32 [8, 4], replicated, may hold values from 0 to 7
- pair_weight: float32 [8, 4], replicated, may hold values from 0.1 to 0.4
- phonon_offset: int32 [4], replicated, may hold values from 1 to 4, as said below
- occupation: float32 [4], replicated, may hold values from 0.2 to 3
- vertex: bfloat16 [4, 8, 64, 64], replicated, may hold values from -0.75 to 0.75
- block_atoms: int32 [2, 2], replicated, may hold values from 0 to 7
Outputs:
- self_energy: bfloat16 [8, 512, 2, 2, 64, 128], P('mom', 'en')
The draws below stay inside these ranges and needn't reach their ends.
Inputs may be any that keep to these rules, and one draw needn't show every extreme that they name: `phonon_offset`: every mode's offset lies in 1 to 4, and some mode's offset is 4.
All inputs are finite; a program needn't handle non-finite values.
Results may differ from the reference program's by a relative error of at most 0.015.
Values may be sent and summed in bfloat16 or wider, within the bound.
No kernel may reach another device: no remote copies, remote signals or barrier semaphores. Data moves between devices by JAX's collectives and lax.ppermute only.
A program may use at most 64 MiB of HBM per device.

```python
import math
import jax
import jax.numpy as jnp
from jax import lax

NORB = 64
NMODE = 4
NATOM = 8
NBLK = 2
PAIRS = 4
OFF_MAX = 4
NK = 8
NE = 512


def draw_phonon_offset(key, part):
    first, second = jax.random.split(jax.random.fold_in(key, 7))
    values = jax.random.randint(first, (NMODE,), 1, OFF_MAX + 1)
    chosen = jax.random.randint(second, (), 0, NMODE)
    return jnp.where(jnp.arange(NMODE) == chosen, OFF_MAX, values).astype(jnp.int32)


def with_ends(values, rng, low, top_value):
    longest = values.shape.index(max(values.shape))
    spots = []
    for shift in (0, 1):
        where = [jax.random.randint(jax.random.fold_in(rng, axis), (), 0, length) for axis, length in enumerate(values.shape)]
        where[longest] = (where[longest] + shift) % values.shape[longest]
        spots.append(tuple(where))
    return values.at[spots[0]].set(low).at[spots[1]].set(top_value)


def level_of(rng, extent, cuts, low, high):
    loudness, own = 1.0, jax.random.fold_in(rng, 6)
    for dim, shards_of in cuts:
        draws = jnp.exp(jax.random.uniform(jax.random.fold_in(own, dim), (shards_of,), jnp.float32, low / len(cuts), high / len(cuts)))
        loudness = loudness * jnp.repeat(draws, extent[dim] // shards_of).reshape([-1 if axis == dim else 1 for axis in range(len(extent))])
    return loudness


def gaussian(own_key, dims, scale, bound, cuts=(), kind=jnp.bfloat16):
    result = scale * jax.random.normal(own_key, dims, jnp.float32)
    if cuts:
        result = result * level_of(own_key, dims, cuts, -0.22, 0.18)
    return jnp.clip(result, -bound, bound).astype(kind)


def setup_inputs(seed: int = 0) -> dict:
    seeds = jax.random.split(jax.random.key(seed), 8)
    return {
        "green": gaussian(seeds[0], (NK, NE, NBLK, 2, NORB, 2 * NORB), 1.0, 6.0, ((0, 8), (1, 64))),
        "pair_index": with_ends(jax.random.randint(seeds[1], (NK, PAIRS), 0, NK), jax.random.fold_in(seeds[1], 1), 0, NK - 1).astype(jnp.int32),
        "pair_weight": jnp.clip(jax.random.uniform(seeds[2], (NK, PAIRS), jnp.float32, 0.1, 0.4), 0.1, 0.4),
        "phonon_offset": draw_phonon_offset(jax.random.fold_in(seeds[7], 71), 0),
        "occupation": jnp.clip(jnp.exp(jax.random.uniform(seeds[4], (NMODE,), jnp.float32, math.log(0.2), math.log(3.0))), 0.2, 3.0),
        "vertex": gaussian(seeds[5], (NMODE, NATOM, NORB, NORB), NORB ** -0.5, 0.75),
        "block_atoms": with_ends(jax.random.randint(seeds[6], (NBLK, 2), 0, NATOM), jax.random.fold_in(seeds[6], 1), 0, NATOM - 1).astype(jnp.int32),
    }


def reference(green, pair_index, pair_weight, phonon_offset, occupation, vertex, block_atoms):
    paired = jnp.zeros(green.shape, jnp.float32)
    for j in range(PAIRS):
        picked = green[pair_index[:, j].astype(jnp.int32)].astype(jnp.float32)
        paired = paired + pair_weight[:, j][:, None, None, None, None, None] * picked
    paired = paired.astype(jnp.bfloat16)
    padding = jnp.zeros((NK, OFF_MAX) + green.shape[2:], jnp.bfloat16)
    extended = jnp.concatenate([padding, paired, padding], axis=1)
    total = jnp.zeros((NK, NE, NBLK, 2, NORB, 2, NORB), jnp.float32)
    for m in range(NMODE):
        shift_by = phonon_offset[m].astype(jnp.int32)
        plus = lax.dynamic_slice_in_dim(extended, OFF_MAX + shift_by, NE, 1).astype(jnp.float32)
        minus = lax.dynamic_slice_in_dim(extended, OFF_MAX - shift_by, NE, 1).astype(jnp.float32)
        bose = occupation[m]
        lesser = (bose + 1.0) * plus[:, :, :, 0] + bose * minus[:, :, :, 0]
        greater = bose * plus[:, :, :, 1] + (bose + 1.0) * minus[:, :, :, 1]
        source = jnp.stack([lesser, greater], axis=3).astype(jnp.bfloat16)
        left_block = vertex[m][block_atoms[:, 0].astype(jnp.int32)].astype(jnp.float32)
        right_block = vertex[m][block_atoms[:, 1].astype(jnp.int32)].astype(jnp.float32)
        half = jnp.einsum("bij,kebtjc->kebtic", left_block, source.astype(jnp.float32)).astype(jnp.bfloat16)
        parts = half.reshape((NK, NE, NBLK, 2, NORB, 2, NORB)).astype(jnp.float32)
        total = total + jnp.einsum("kebtipj,blj->kebtipl", parts, right_block)
    return total.reshape(green.shape).astype(jnp.bfloat16)
```

```python
import jax
import jax.numpy as jnp
from jax import lax
from jax.experimental import pallas as pl
from jax.experimental.pallas import tpu as pltpu
from jax.sharding import PartitionSpec as P

OFF_MAX = 4
VMEM = pltpu.MemorySpace.VMEM
SMEM = pltpu.MemorySpace.SMEM
VMEM_LIMIT = 24 * 2**20


def weights_body(atoms, vertex, left, right):
    nblk, modes, norb = left.shape[0], vertex.shape[0], vertex.shape[-1]
    left[...] = jnp.zeros_like(left)
    right[...] = jnp.zeros_like(right)
    for b in range(nblk):
        for m in range(modes):
            span = slice(m * norb, (m + 1) * norb)
            left[b, span, span] = vertex[m, atoms[b, 0]]
            block = vertex[m, atoms[b, 1]]
            for p in range(2):
                start = (2 * m + p) * norb
                right[b, p * norb : (p + 1) * norb, start : start + norb] = block


def weights(block_atoms, vertex):
    modes, _, norb, _ = vertex.shape
    nblk = block_atoms.shape[0]
    return pl.pallas_call(
        weights_body,
        out_shape=(
            jax.ShapeDtypeStruct((nblk, modes * norb, modes * norb), vertex.dtype),
            jax.ShapeDtypeStruct((nblk, 2 * norb, modes * 2 * norb), vertex.dtype),
        ),
        in_specs=[pl.BlockSpec(memory_space=SMEM), pl.BlockSpec(memory_space=VMEM)],
        out_specs=(pl.BlockSpec(memory_space=VMEM), pl.BlockSpec(memory_space=VMEM)),
        compiler_params=pltpu.CompilerParams(vmem_limit_bytes=VMEM_LIMIT),
        name="weights",
    )(block_atoms, vertex)


def mix_body(index, weight, spread, summed):
    for k in range(summed.shape[0]):
        for b in range(summed.shape[1]):
            for t in range(summed.shape[2]):
                total = weight[k, 0] * spread[index[k, 0], b, t].astype(jnp.float32)
                for j in range(1, index.shape[1]):
                    total = total + weight[k, j] * spread[index[k, j], b, t].astype(jnp.float32)
                summed[k, b, t] = total.astype(summed.dtype)


def mix(pair_index, pair_weight, spread):
    smem = pl.BlockSpec(memory_space=SMEM)
    vmem = pl.BlockSpec(memory_space=VMEM)
    return pl.pallas_call(
        mix_body,
        out_shape=jax.ShapeDtypeStruct((pair_index.shape[0],) + spread.shape[1:], spread.dtype),
        in_specs=[smem, smem, vmem],
        out_specs=vmem,
        cost_estimate=pl.CostEstimate(
            flops=8 * spread.size, bytes_accessed=4 * spread.size, transcendentals=0
        ),
        compiler_params=pltpu.CompilerParams(vmem_limit_bytes=VMEM_LIMIT),
        name="mix",
    )(pair_index, pair_weight, spread)


def scatter_body(offset, bose, edge, below, own, above, far, left, right, out, ext, source, half):
    e_local, norb, width = own.shape[0], own.shape[3], own.shape[4]
    modes = offset.shape[0]
    ext[:OFF_MAX] = below[...]
    ext[OFF_MAX : OFF_MAX + e_local] = own[...]
    ext[OFF_MAX + e_local :] = above[...]

    @pl.when(edge[0] == 1)
    def _():
        ext[OFF_MAX + e_local :] = far[...]

    @pl.when(edge[0] == 2)
    def _():
        ext[:OFF_MAX] = far[...]

    for b in range(own.shape[1]):
        for t in range(own.shape[2]):
            for m in range(modes):
                n = bose[m]
                up, down = (n + 1.0, n) if t == 0 else (n, n + 1.0)
                for e in range(e_local):
                    plus = ext[OFF_MAX + e + offset[m], b, t].astype(jnp.float32)
                    minus = ext[OFF_MAX + e - offset[m], b, t].astype(jnp.float32)
                    source[m * norb : (m + 1) * norb, e * width : (e + 1) * width] = (
                        up * plus + down * minus
                    ).astype(source.dtype)
            product = jnp.dot(left[b], source[...], preferred_element_type=jnp.float32)
            product = product.astype(half.dtype)
            for m in range(modes):
                for e in range(e_local):
                    half[e * norb : (e + 1) * norb, m * width : (m + 1) * width] = product[
                        m * norb : (m + 1) * norb, e * width : (e + 1) * width
                    ]
            total = lax.dot_general(
                half[...], right[b], (((1,), (1,)), ((), ())), preferred_element_type=jnp.float32
            )
            out[0, :, b, t] = total.reshape(e_local, norb, width).astype(out.dtype)


def scatter(shape, offset, bose, edge, below, own, above, far, left, right):
    e_local, nblk, _, norb, width = own.shape
    modes = offset.shape[0]
    smem = pl.BlockSpec(memory_space=SMEM)
    vmem = pl.BlockSpec(memory_space=VMEM)
    return pl.pallas_call(
        scatter_body,
        out_shape=jax.ShapeDtypeStruct(shape, own.dtype),
        in_specs=[smem] * 3 + [vmem] * 6,
        out_specs=vmem,
        scratch_shapes=[
            pltpu.VMEM((e_local + 2 * OFF_MAX,) + own.shape[1:], own.dtype),
            pltpu.VMEM((modes * norb, e_local * width), own.dtype),
            pltpu.VMEM((e_local * norb, modes * width), own.dtype),
        ],
        compiler_params=pltpu.CompilerParams(vmem_limit_bytes=VMEM_LIMIT),
        cost_estimate=pl.CostEstimate(
            flops=2**31, bytes_accessed=8 * own.size, transcendentals=0
        ),
        name="scatter",
    )(offset, bose, edge, below, own, above, far, left, right)


def local(green, pair_index, pair_weight, phonon_offset, occupation, vertex, block_atoms):
    left, right = weights(block_atoms, vertex)
    spread = lax.all_to_all(green[0], "mom", split_axis=0, concat_axis=0, tiled=True)
    summed = mix(pair_index, pair_weight, spread)
    own = lax.all_to_all(summed, "mom", split_axis=0, concat_axis=0, tiled=True)
    last = lax.axis_size("en")
    cut = last // 2
    en = lax.axis_index("en")
    high, low = own[own.shape[0] - OFF_MAX :], own[:OFF_MAX]
    edge = jnp.where(en == cut - 1, 1, jnp.where(en == cut, 2, 0)).astype(jnp.int32).reshape(1)
    far = lax.ppermute(
        jnp.where(en == cut - 1, high, low), "en", [(cut - 1, cut), (cut, cut - 1)]
    )
    below = lax.ppermute(high, "en", [(i - 1, i) for i in range(1, last) if i != cut])
    above = lax.ppermute(low, "en", [(i, i - 1) for i in range(1, last) if i != cut])
    return scatter(
        green.shape, phonon_offset, occupation, edge, below, own, above, far, left, right
    )


def solution(mesh):
    in_specs = (P("mom", "en", None, None, None, None), P(), P(), P(), P(), P(), P())
    out_specs = P("mom", "en", None, None, None, None)
    return jax.shard_map(local, mesh=mesh, in_specs=in_specs, out_specs=out_specs, check_vma=False)
```

```python
import jax
import jax.numpy as jnp
from jax import lax
from jax.experimental import pallas as pl
from jax.experimental.pallas import tpu as pltpu
from jax.sharding import PartitionSpec as P


OFF_MAX = 4
VMEM = pltpu.MemorySpace.VMEM
SMEM = pltpu.MemorySpace.SMEM
UP_ORDER = (4, 3, 5, 2, 6, 1, 7, 0)
DOWN_ORDER = (0, 1, 7, 2, 6, 3, 5, 4)
VMEM_LIMIT = 24 * 2**20


def weights_body(atoms, vertex, left, right):
    nblk, modes, norb = left.shape[0], vertex.shape[0], vertex.shape[-1]
    left[...] = jnp.zeros_like(left)
    right[...] = jnp.zeros_like(right)
    for b in range(nblk):
        for m in range(modes):
            span = slice(m * norb, (m + 1) * norb)
            left[b, span, span] = vertex[m, atoms[b, 0]]
            block = vertex[m, atoms[b, 1]]
            for p in range(2):
                start = (2 * m + p) * norb
                right[b, p * norb : (p + 1) * norb, start : start + norb] = block


def weights(block_atoms, vertex):
    modes, _, norb, _ = vertex.shape
    nblk = block_atoms.shape[0]
    return pl.pallas_call(
        weights_body,
        out_shape=(
            jax.ShapeDtypeStruct((nblk, modes * norb, modes * norb), vertex.dtype),
            jax.ShapeDtypeStruct((nblk, 2 * norb, modes * 2 * norb), vertex.dtype),
        ),
        in_specs=[pl.BlockSpec(memory_space=SMEM), pl.BlockSpec(memory_space=VMEM)],
        out_specs=(pl.BlockSpec(memory_space=VMEM), pl.BlockSpec(memory_space=VMEM)),
        compiler_params=pltpu.CompilerParams(vmem_limit_bytes=VMEM_LIMIT),
        name="weights",
    )(block_atoms, vertex)


def crossing():
    en, cut = lax.axis_index("en"), lax.axis_size("en") // 2
    return en == cut - 1, en == cut


def mix_body(index, weight, spread, summed, *pieces):
    for k in range(summed.shape[0]):
        for b in range(summed.shape[1]):
            for t in range(summed.shape[2]):
                total = weight[k, 0] * spread[index[k, 0], b, t].astype(jnp.float32)
                for j in range(1, index.shape[1]):
                    total = total + weight[k, j] * spread[index[k, j], b, t].astype(jnp.float32)
                summed[k, b, t] = total.astype(summed.dtype)
    low_side, high_side = crossing()

    @pl.when(low_side | high_side)
    def _():
        for s, piece in enumerate(pieces):
            piece[...] = summed[lax.rem(lax.axis_index("mom") + s, len(pieces))]


def mix(pair_index, pair_weight, spread):
    smem = pl.BlockSpec(memory_space=SMEM)
    vmem = pl.BlockSpec(memory_space=VMEM)
    count = pair_index.shape[0]
    piece = jax.ShapeDtypeStruct(spread.shape[1:], spread.dtype)
    return pl.pallas_call(
        mix_body,
        out_shape=[jax.ShapeDtypeStruct((count,) + spread.shape[1:], spread.dtype)]
        + [piece] * count,
        in_specs=[smem, smem, vmem],
        out_specs=[vmem] * (1 + count),
        cost_estimate=pl.CostEstimate(
            flops=8 * spread.size, bytes_accessed=4 * spread.size, transcendentals=0
        ),
        compiler_params=pltpu.CompilerParams(vmem_limit_bytes=VMEM_LIMIT),
        name="mix",
    )(pair_index, pair_weight, spread)


def scatter_body(offset, bose, below, own, above, *rest):
    count = (len(rest) - 6) // 2
    up, down = rest[:count], rest[count : 2 * count]
    left, right, out, ext, source, half = rest[2 * count :]
    e_local, norb, width = own.shape[0], own.shape[3], own.shape[4]
    modes = offset.shape[0]
    ext[:OFF_MAX] = below[...]
    ext[OFF_MAX : OFF_MAX + e_local] = own[...]
    ext[OFF_MAX + e_local :] = above[...]
    low_side, high_side = crossing()
    for s in range(count):
        origin = lax.rem(lax.axis_index("mom") - s + count, count)

        @pl.when(high_side & (origin >= e_local - OFF_MAX))
        def _():
            ext[origin - (e_local - OFF_MAX)] = up[s][...]

        @pl.when(low_side & (origin < OFF_MAX))
        def _():
            ext[OFF_MAX + e_local + origin] = down[s][...]

    for b in range(own.shape[1]):
        for t in range(own.shape[2]):
            for m in range(modes):
                n = bose[m]
                up, down = (n + 1.0, n) if t == 0 else (n, n + 1.0)
                for e in range(e_local):
                    plus = ext[OFF_MAX + e + offset[m], b, t].astype(jnp.float32)
                    minus = ext[OFF_MAX + e - offset[m], b, t].astype(jnp.float32)
                    source[m * norb : (m + 1) * norb, e * width : (e + 1) * width] = (
                        up * plus + down * minus
                    ).astype(source.dtype)
            product = jnp.dot(left[b], source[...], preferred_element_type=jnp.float32)
            product = product.astype(half.dtype)
            for m in range(modes):
                for e in range(e_local):
                    half[e * norb : (e + 1) * norb, m * width : (m + 1) * width] = product[
                        m * norb : (m + 1) * norb, e * width : (e + 1) * width
                    ]
            total = lax.dot_general(
                half[...], right[b], (((1,), (1,)), ((), ())), preferred_element_type=jnp.float32
            )
            out[0, :, b, t] = total.reshape(e_local, norb, width).astype(out.dtype)


def scatter(shape, offset, bose, below, own, above, up, down, left, right):
    e_local, _, _, norb, width = own.shape
    modes = offset.shape[0]
    smem = pl.BlockSpec(memory_space=SMEM)
    vmem = pl.BlockSpec(memory_space=VMEM)
    args = (below, own, above, *up, *down, left, right)
    return pl.pallas_call(
        scatter_body,
        out_shape=jax.ShapeDtypeStruct(shape, own.dtype),
        in_specs=[smem] * 2 + [vmem] * len(args),
        out_specs=vmem,
        scratch_shapes=[
            pltpu.VMEM((e_local + 2 * OFF_MAX,) + own.shape[1:], own.dtype),
            pltpu.VMEM((modes * norb, e_local * width), own.dtype),
            pltpu.VMEM((e_local * norb, modes * width), own.dtype),
        ],
        compiler_params=pltpu.CompilerParams(vmem_limit_bytes=VMEM_LIMIT),
        cost_estimate=pl.CostEstimate(
            flops=2**31, bytes_accessed=8 * own.size, transcendentals=0
        ),
        name="scatter",
    )(offset, bose, *args)


def local(green, pair_index, pair_weight, phonon_offset, occupation, vertex, block_atoms):
    left, right = weights(block_atoms, vertex)
    spread = lax.all_to_all(green[0], "mom", split_axis=0, concat_axis=0, tiled=True)
    summed, *pieces = mix(pair_index, pair_weight, spread)
    own = lax.all_to_all(summed, "mom", split_axis=0, concat_axis=0, tiled=True)
    count, last = lax.axis_size("mom"), lax.axis_size("en")
    cut, e_local = last // 2, own.shape[0]
    ups, downs = range(e_local - OFF_MAX, e_local), range(OFF_MAX)
    up, down = [None] * count, [None] * count
    for s in UP_ORDER:
        route = [(m * last + cut - 1, (m + s) % count * last + cut) for m in ups]
        up[s] = lax.ppermute(pieces[s], ("mom", "en"), route)
    for s in DOWN_ORDER:
        route = [(m * last + cut, (m + s) % count * last + cut - 1) for m in downs]
        down[s] = lax.ppermute(pieces[s], ("mom", "en"), route)
    high, low = own[e_local - OFF_MAX :], own[:OFF_MAX]
    below = lax.ppermute(high, "en", [(i - 1, i) for i in range(1, last) if i != cut])
    above = lax.ppermute(low, "en", [(i, i - 1) for i in range(1, last) if i != cut])
    return scatter(
        green.shape,
        phonon_offset,
        occupation,
        below,
        own,
        above,
        up,
        down,
        left,
        right,
    )


def solution(mesh):
    in_specs = (P("mom", "en", None, None, None, None), P(), P(), P(), P(), P(), P())
    out_specs = P("mom", "en", None, None, None, None)
    return jax.shard_map(local, mesh=mesh, in_specs=in_specs, out_specs=out_specs, check_vma=False)
```
